128 devices in a mesh: dom: 4 (over z), rows: 32 (over y, x, core).
Axes of the slice: x: 4, y: 4, z: 4, core: 2. Of those that a mesh axis runs over, the one named last changes fastest.
Arguments:
- blocks: bfloat16 [2048, 6, 128, 128], P('rows'), may hold values from -0.15625 to 0.15625
- columns: int32 [2048, 6], P('rows'), may hold values from 0 to 2047, as said below
- counts: int32 [32], P('rows'), may hold values from 2 to 64, as said below
- start_block: float32 [2048, 2, 32, 128], P('rows'), may hold values from -6 to 6
- shift_radius: float32 [8], P('dom'), parts along dimension 0, may hold values from 1 to 1.25
- shift_angle: float32 [8], P('dom'), parts along dimension 0, may hold values from -3.140625 to 3.140625
Outputs:
- solution: float32 [8192, 2, 64, 128], P(('dom', 'rows')), parts along dimension 0
The draws below stay inside these ranges and needn't reach their ends.
There are 4 independent parts, one for each index of `dom`. The reference program is written for one: setup_inputs(seed, part) draws one part's arguments, and reference() takes and returns one part's arrays. A program takes and returns all parts, laid end to end along the dimension named above; an argument that names none is the same for every part. Nothing has to cross between parts.
Inputs may be any that keep to these rules, and one draw needn't show every extreme that they name: `counts`: live block-rows of each device; some device has all 64 live. `columns`: A live block-row i of device d lists first i itself, then three live block-rows of d, then two block-rows among the first 2 of devices other than d. A dead block-row lists only itself.
All inputs are finite; a program needn't handle non-finite values.
Results may differ from the reference program's by a relative error of at most 0.0038.
Values may be sent and summed in bfloat16 or wider, within the bound.
No kernel may reach another device: no remote copies, remote signals or barrier semaphores. Data moves between devices by JAX's collectives and lax.ppermute only.
A program may use at most 128 MiB of HBM per device.

```python
import math
import jax
import jax.numpy as jnp

BS = 128
NNZB = 6
NVEC = 16
SHIFTS = 2
HB = 2
ITERS = 4
CAP = 64
OWNERS = 32
NBR = 2048


def structure(key):
    spread = CAP - HB
    first_draw = jax.random.randint(jax.random.fold_in(key, 101), (OWNERS,), 0, spread + 1)
    second = jax.random.randint(jax.random.fold_in(key, 102), (OWNERS,), 0, spread + 1)
    counts = HB + first_draw * second // spread
    chosen = jax.random.randint(jax.random.fold_in(key, 103), (), 0, OWNERS)
    counts = jnp.where(jnp.arange(OWNERS) == chosen, CAP, counts).astype(jnp.int32)
    row_ids = jnp.arange(NBR, dtype=jnp.int32)
    owner_dev = row_ids // CAP
    slot_pos = row_ids % CAP
    alive_count = counts[owner_dev]
    near_cols = jax.random.randint(jax.random.fold_in(key, 104), (NBR, 3), 0, 1 << 20) % alive_count[:, None] + owner_dev[:, None] * CAP
    hop_count = jax.random.randint(jax.random.fold_in(key, 105), (NBR, 2), 1, OWNERS)
    hop_first = jnp.where(slot_pos == 1, 1, hop_count[:, 0])
    hop_second = jnp.where(slot_pos == 0, OWNERS // 2, hop_count[:, 1])
    hop_count = jnp.stack([hop_first, hop_second], 1)
    far_dev = (owner_dev[:, None] + hop_count) % OWNERS
    far_slot = jax.random.randint(jax.random.fold_in(key, 106), (NBR, 2), 0, HB)
    far_cols = far_dev * CAP + far_slot
    listed = jnp.concatenate([row_ids[:, None], near_cols, far_cols], 1)
    listed = jnp.where((slot_pos < alive_count)[:, None], listed, row_ids[:, None])
    return (counts, listed.astype(jnp.int32))


def draw_columns(key, part):
    return structure(key)[1]


def draw_counts(key, part):
    return structure(key)[0]


def block_levels(rng, dims, shards, least, top_value):
    level = 1.0
    for dim, blocks in shards:
        heights = jax.random.uniform(jax.random.fold_in(jax.random.fold_in(rng, 6), dim), (blocks,), jnp.float32, least / len(shards), top_value / len(shards))
        level = level * jnp.repeat(jnp.exp(heights), dims[dim] // blocks).reshape((-1,) + (1,) * (len(dims) - 1 - dim))
    return level


def centred(stream_key, dims, scale, limit, pieces=(), kind=jnp.bfloat16):
    entries = scale * jax.random.normal(stream_key, dims, jnp.float32)
    if pieces:
        entries = entries * block_levels(stream_key, dims, pieces, -0.22, 0.18)
    return jnp.clip(entries, -limit, limit).astype(kind)


def setup_inputs(seed: int = 0, part: int = 0) -> dict:
    keys = jax.random.split(jax.random.key(seed), 7)
    part_keys = jax.random.split(jax.random.fold_in(keys[6], part), 7)
    blocks = centred(keys[0], (NBR, NNZB, BS, BS), (2 * NNZB * BS) ** -0.5, 0.15625, ((0, 32),))
    columns = draw_columns(jax.random.fold_in(keys[6], 71), part)
    counts = draw_counts(jax.random.fold_in(keys[6], 71), part)
    start_block = centred(keys[3], (NBR, 2, 2 * NVEC, BS), 1.0, 6.0, ((0, 32),), jnp.float32)
    shift_radius = jnp.clip(jnp.exp(jax.random.uniform(part_keys[4], (SHIFTS,), jnp.float32, math.log(1.0), math.log(1.25))), 1.0, 1.25)
    shift_angle = jnp.clip(jax.random.uniform(part_keys[5], (SHIFTS,), jnp.float32, -3.140625, 3.140625), -3.140625, 3.140625)
    return dict(blocks=blocks, columns=columns, counts=counts, start_block=start_block, shift_radius=shift_radius, shift_angle=shift_angle)


def rotate(values, weight_re, weight_im):
    row_count = values.shape[0]
    grouped = values.reshape(row_count, 2, weight_re.shape[0], 2, -1, values.shape[-1])
    real_part = grouped[:, :, :, 0]
    imag_part = grouped[:, :, :, 1]
    scale_re = weight_re[None, None, :, None, None]
    scale_im = weight_im[None, None, :, None, None]
    out_re = scale_re * real_part - scale_im * imag_part
    out_im = scale_re * imag_part + scale_im * real_part
    return jnp.stack([out_re, out_im], 3).reshape(values.shape)


def reference(blocks, columns, counts, start_block, shift_radius, shift_angle):
    block_rows = blocks.shape[0]
    row_ids = jnp.arange(block_rows, dtype=jnp.int32)
    owner_dev = row_ids // CAP
    alive_rows = ((row_ids % CAP) < counts[owner_dev]).astype(jnp.float32)
    source = start_block * alive_rows[:, None, None, None]
    width = start_block.shape[-1]
    driven = jnp.broadcast_to(source[:, :, None], (block_rows, 2, SHIFTS, 2 * NVEC, width)).reshape(block_rows, 2, SHIFTS * 2 * NVEC, width)
    weight_re = jnp.cos(shift_angle) / shift_radius
    weight_im = -jnp.sin(shift_angle) / shift_radius
    tiles = blocks.astype(jnp.float32)
    iterate = rotate(driven, weight_re, weight_im)
    for counter in range(ITERS):
        packed = iterate.astype(jnp.bfloat16).astype(jnp.float32)
        upper_half = packed[:, 0]
        lower_half = packed[:, 1]
        picked = lower_half[columns]
        top_part = jnp.einsum("knab,kncb->kca", tiles, picked) * alive_rows[:, None, None]
        partial_terms = jnp.einsum("knab,kca->kncb", tiles, upper_half)
        bottom = jax.ops.segment_sum(partial_terms.reshape(-1, partial_terms.shape[2], width), columns.reshape(-1), num_segments=block_rows)
        iterate = rotate(driven + jnp.stack([top_part, bottom], 1), weight_re, weight_im)
    return iterate
```

```python
import functools

import jax
import jax.numpy as jnp
from jax import lax
from jax.experimental import pallas as pl
from jax.experimental.pallas import tpu as pltpu
from jax.sharding import PartitionSpec as P


HB = 2
RB = 8
F32 = jnp.float32
BF16 = jnp.bfloat16


def split(value):
    high = value.astype(BF16)
    low = (value - high.astype(F32)).astype(BF16)
    return jnp.concatenate([high, low], 0)


def fold(value):
    half = value.shape[0] // 2
    return value[:half] + value[half:]


def forward(block_ref, rows, r):
    total = None
    for m in range(3):
        lhs = jnp.concatenate([rows[2 * m], rows[2 * m + 1]], 1)
        rhs = jnp.concatenate([block_ref[r, 2 * m], block_ref[r, 2 * m + 1]], 1)
        term = lax.dot_general(lhs, rhs, (((1,), (1,)), ((), ())), preferred_element_type=F32)
        total = term if total is None else total + term
    return fold(total)


def backward(block_ref, both, r):
    out = []
    for m in range(3):
        rhs = jnp.concatenate([block_ref[r, 2 * m], block_ref[r, 2 * m + 1]], 1)
        term = fold(jnp.dot(both, rhs, preferred_element_type=F32))
        width = term.shape[1] // 2
        out += [term[:, :width], term[:, width:]]
    return out


def scatter(idx_ref, far_at, block_ref, both, r, row, acc_ref, part_ref):
    terms = backward(block_ref, both, r)
    acc_ref[row] += terms[0]
    for n in range(3):
        acc_ref[idx_ref[row * 7 + n]] += terms[1 + n]
    for n in range(2):
        part_ref[idx_ref[row * 7 + far_at + n]] += terms[4 + n]


def mix(coef_ref, rows):
    out = []
    half = rows[0].shape[0] // 2
    for p in range(2):
        re = im = None
        for k, value in enumerate(rows):
            a = coef_ref[p * 10 + k]
            b = coef_ref[p * 10 + 5 + k]
            vr, vi = value[:half], value[half:]
            tr, ti = a * vr - b * vi, a * vi + b * vr
            re = tr if re is None else re + tr
            im = ti if im is None else im + ti
        out += [re, im]
    return jnp.concatenate(out, 0)


def finish(sc_ref, own_at, acc_ref, part_ref, keep_ref, send_ref):
    half = keep_ref.shape[0]
    own = sc_ref[own_at] * HB
    for s in range(HB):
        part_ref[own + s] += acc_ref[s]
    for j in range(0, half, 8):
        keep_ref[pl.ds(j, 8)] = part_ref[pl.ds(j, 8)]
        send_ref[pl.ds(j, 8)] = part_ref[pl.ds(half + j, 8)].astype(BF16)


def first_kernel(far_at, own_at, idx_ref, sc_ref, block_ref, drive_ref, acc_ref, keep_ref, send_ref, part_ref):
    i = pl.program_id(0)
    count = sc_ref[0]

    @pl.when(i == 0)
    def _():
        acc_ref[...] = jnp.zeros_like(acc_ref)
        part_ref[...] = jnp.zeros_like(part_ref)

    @pl.when(i * RB < count)
    def _():
        for r in range(RB):
            row = i * RB + r
            value = jnp.where(row < count, drive_ref[r, 0], 0.0)
            scatter(idx_ref, far_at, block_ref, split(value), r, row, acc_ref, part_ref)

    @pl.when(i == pl.num_programs(0) - 1)
    def _():
        finish(sc_ref, own_at, acc_ref, part_ref, keep_ref, send_ref)


def load_rows(local, local_ref, table_refs, rows_ref, table_ref, own):
    for j in range(rows_ref.shape[0]):
        rows_ref[j] = split(local_ref[j, 0] if local else local_ref[j])
    width = table_refs[0].shape[1]
    if len(table_refs) == 1:
        for j in range(table_ref.shape[0]):
            value = table_refs[0][j]
            table_ref[j] = jnp.concatenate([value, jnp.zeros_like(value)], 0)
    else:
        half = table_refs[0].shape[0]
        for j in range(half):
            table_ref[j] = split(table_refs[0][j])
            value = table_refs[1][j]
            table_ref[half + j] = jnp.concatenate([value, jnp.zeros_like(value)], 0)
        for s in range(HB):
            rows_ref[s] = table_ref[own + s]


def product(idx_ref, read_at, block_ref, rows_ref, table_ref, r, row, count):
    rows = [rows_ref[row]]
    rows += [rows_ref[idx_ref[row * 7 + n]] for n in range(3)]
    rows += [table_ref[idx_ref[row * 7 + read_at + n]] for n in range(2)]
    return jnp.where(row < count, forward(block_ref, rows, r), 0.0)


def middle_kernel(tables, read_at, read_own, far_at, own_at, idx_ref, sc_ref, block_ref, local_ref, *refs):
    table_refs = refs[:tables]
    up_ref, acc_ref, keep_ref, send_ref, rows_ref, table_ref, part_ref = refs[tables:]
    i = pl.program_id(0)
    count = sc_ref[0]

    @pl.when(i == 0)
    def _():
        acc_ref[...] = jnp.zeros_like(acc_ref)
        part_ref[...] = jnp.zeros_like(part_ref)
        load_rows(tables == 1, local_ref, table_refs, rows_ref, table_ref, sc_ref[read_own] * HB)

    @pl.when(i * RB < count)
    def _():
        both = []
        for r in range(RB):
            row = i * RB + r
            value = product(idx_ref, read_at, block_ref, rows_ref, table_ref, r, row, count)
            up_ref[r] = value
            both.append(split(value))
        for r in range(RB):
            scatter(idx_ref, far_at, block_ref, both[r], r, i * RB + r, acc_ref, part_ref)

    @pl.when(i * RB >= count)
    def _():
        up_ref[...] = jnp.zeros_like(up_ref)

    @pl.when(i == pl.num_programs(0) - 1)
    def _():
        finish(sc_ref, own_at, acc_ref, part_ref, keep_ref, send_ref)


def last_kernel(read_at, read_own, idx_ref, sc_ref, block_ref, local_ref, keep_ref, recv_ref, coef_ref,
                drive_ref, u1_ref, u2_ref, u3_ref, out_ref, rows_ref, table_ref):
    i = pl.program_id(0)
    count = sc_ref[0]

    @pl.when(i == 0)
    def _():
        load_rows(False, local_ref, (keep_ref, recv_ref), rows_ref, table_ref, sc_ref[read_own] * HB)

    @pl.when(i * RB < count)
    def _():
        for r in range(RB):
            row = i * RB + r
            value = product(idx_ref, read_at, block_ref, rows_ref, table_ref, r, row, count)
            drive = jnp.where(row < count, drive_ref[r, 0], 0.0)
            out_ref[r, 0] = mix(coef_ref, [drive, u1_ref[r], u2_ref[r], u3_ref[r], value])

    @pl.when(i * RB >= count)
    def _():
        out_ref[...] = jnp.zeros_like(out_ref)


def lower_kernel(sc_ref, coef_ref, drive_ref, l1_ref, l2_ref, l3_ref, l4_ref, held_ref, out_ref):
    i = pl.program_id(0)
    count = sc_ref[0]
    for r in range(RB):
        drive = jnp.where(i * RB + r < count, drive_ref[r, 0], 0.0)
        out_ref[r, 0] = mix(coef_ref, [drive, l1_ref[r], l2_ref[r], l3_ref[r], l4_ref[r]])


def leading_kernel(sc_ref, coef_ref, drive_ref, k1_ref, k2_ref, k3_ref, k4_ref, held_ref, out_ref):
    for s in range(HB):
        out_ref[s, 0] = mix(coef_ref, [drive_ref[s, 0], k1_ref[s], k2_ref[s], k3_ref[s], k4_ref[s]])


def exchanges():
    def pairs(partner):
        found = []
        for i in range(32):
            c, x, y = partner(i & 1, (i >> 1) & 3, i >> 3)
            found.append((i, c | (x << 1) | (y << 3)))
        return found

    def chip(bit, first):
        def partner(c, x, y):
            if (c == 0) == first:
                return c, x ^ bit, y
            return c, x, y ^ bit
        return pairs(partner)

    core = pairs(lambda c, x, y: (c ^ 1, x, y))
    return core, [chip(1, True), chip(3, True), chip(1, False), chip(3, False)]


def body(blocks, columns, counts, start_block, shift_radius, shift_angle):
    slots, stored, bs, _ = blocks.shape
    cols = start_block.shape[2]
    owners = lax.axis_size("rows")
    table = owners * HB
    half = table // 2
    me = lax.axis_index("rows")
    core, steps = exchanges()

    owner = columns // slots
    within = columns - owner * slots
    lead = jnp.minimum(within, HB - 1)
    off = owner ^ me
    rc, rx, ry = off & 1, (off >> 1) & 3, off >> 3

    def bits(value):
        return 2 * ((value ^ (value >> 1)) & 1) + (value >> 1)

    bx, by = bits(rx), bits(ry)
    relative = 16 * rc + jnp.where((owner & 1) == 0, 4 * bx + by, 4 * by + bx)
    absolute = 16 * rc + (owner >> 1)
    idx = jnp.concatenate(
        [within[:, 1:4], (absolute * HB + lead)[:, 4:], (relative * HB + lead)[:, 4:]], 1
    ).reshape(-1).astype(jnp.int32)
    sc = jnp.stack([counts[0], (me >> 1).astype(jnp.int32), jnp.int32(0), jnp.int32(0)])
    power = jnp.arange(1, 6, dtype=F32)
    size = shift_radius[:, None] ** (-power)[None]
    turn = shift_angle[:, None] * power[None]
    coef = jnp.concatenate([jnp.cos(turn) * size, -jnp.sin(turn) * size], 1).reshape(-1)

    ABS, REL = 3, 5
    OWN_ABS, OWN_REL = 1, 2
    steps_grid = slots // RB

    def live(i, sc_ref):
        return jnp.minimum(i, (sc_ref[0] - 1) // RB)

    block_spec = pl.BlockSpec((RB, stored, bs, bs), lambda i, ix, sc: (live(i, sc), 0, 0, 0))
    whole = lambda shape: pl.BlockSpec(shape, lambda i, ix, sc: (0,) * len(shape))
    row_spec = pl.BlockSpec((RB, cols, bs), lambda i, ix, sc: (i, 0, 0))
    smem = pl.BlockSpec(memory_space=pltpu.SMEM)
    acc_shape = (slots, cols, bs)
    keep_shape = (half, cols, bs)
    rows_scratch = pltpu.VMEM((slots, 2 * cols, bs), BF16)
    table_scratch = pltpu.VMEM((table, 2 * cols, bs), BF16)
    part_scratch = pltpu.VMEM((table, cols, bs), F32)
    params = pltpu.CompilerParams(dimension_semantics=("arbitrary",), vmem_limit_bytes=40 << 20)
    flops = slots * stored * 2 * bs * bs * 2 * cols

    def cost(passes):
        return pl.CostEstimate(flops=passes * flops, bytes_accessed=blocks.size * 2, transcendentals=0)

    tail_shapes = [
        jax.ShapeDtypeStruct(acc_shape, F32),
        jax.ShapeDtypeStruct(keep_shape, F32),
        jax.ShapeDtypeStruct(keep_shape, BF16),
    ]
    tail_specs = [whole(acc_shape), whole(keep_shape), whole(keep_shape)]

    def first():
        return pl.pallas_call(
            functools.partial(first_kernel, ABS, OWN_ABS),
            grid_spec=pltpu.PrefetchScalarGridSpec(
                num_scalar_prefetch=2,
                grid=(steps_grid,),
                in_specs=[block_spec, pl.BlockSpec((RB, 1, cols, bs), lambda i, ix, sc: (i, 0, 0, 0))],
                out_specs=tail_specs,
                scratch_shapes=[part_scratch],
            ),
            out_shape=tail_shapes,
            compiler_params=params,
            cost_estimate=cost(1),
            name="first",
        )(idx, sc, blocks, start_block)

    def middle(local, tables, read_at, read_own, far_at, own_at, name):
        if local.ndim == 4:
            local_spec = pl.BlockSpec((slots, 1, cols, bs), lambda i, ix, sc: (0, 1, 0, 0))
        else:
            local_spec = whole(acc_shape)
        return pl.pallas_call(
            functools.partial(middle_kernel, len(tables), read_at, read_own, far_at, own_at),
            grid_spec=pltpu.PrefetchScalarGridSpec(
                num_scalar_prefetch=2,
                grid=(steps_grid,),
                in_specs=[block_spec, local_spec] + [whole(t.shape) for t in tables],
                out_specs=[row_spec] + tail_specs,
                scratch_shapes=[rows_scratch, table_scratch, part_scratch],
            ),
            out_shape=[jax.ShapeDtypeStruct(acc_shape, F32)] + tail_shapes,
            compiler_params=params,
            cost_estimate=cost(2),
            name=name,
        )(idx, sc, blocks, local, *tables)

    def everywhere(keep, send):
        keep = keep + lax.ppermute(send, "rows", core)
        for step in steps:
            keep = keep + lax.ppermute(keep.astype(BF16), "rows", step)
        return keep, lax.ppermute(keep.astype(BF16), "rows", core)

    heads = start_block[:HB, 1].astype(BF16)
    for step in reversed(steps):
        heads = jnp.concatenate([heads, lax.ppermute(heads, "rows", step)], 0)
    heads = jnp.concatenate([heads, lax.ppermute(heads, "rows", core)], 0)

    l1, keep, send = first()
    keep1, recv1 = everywhere(keep, send)
    u1, l2, keep, send = middle(start_block, [heads], REL, OWN_REL, ABS, OWN_ABS, "second")
    keep2, recv2 = everywhere(keep, send)
    u2, l3, keep, send = middle(l1, [keep1, recv1], ABS, OWN_ABS, ABS, OWN_ABS, "third")
    keep3, recv3 = everywhere(keep, send)
    u3, l4, keep, send = middle(l2, [keep2, recv2], ABS, OWN_ABS, REL, OWN_REL, "fourth")
    keep = keep + lax.ppermute(send, "rows", core)
    for step in steps:
        size = keep.shape[0] // 2
        keep = keep[:size] + lax.ppermute(keep[size:].astype(BF16), "rows", step)
    keep4 = keep

    out_type = jax.ShapeDtypeStruct((slots, 2, 4 * (cols // 2), bs), F32)
    upper = pl.pallas_call(
        functools.partial(last_kernel, ABS, OWN_ABS),
        grid_spec=pltpu.PrefetchScalarGridSpec(
            num_scalar_prefetch=2,
            grid=(steps_grid,),
            in_specs=[block_spec, whole(acc_shape), whole(keep_shape), whole(keep_shape), smem,
                      pl.BlockSpec((RB, 1, cols, bs), lambda i, ix, sc: (i, 0, 0, 0)),
                      row_spec, row_spec, row_spec],
            out_specs=pl.BlockSpec((RB, 1, 2 * cols, bs), lambda i, ix, sc: (i, 0, 0, 0)),
            scratch_shapes=[rows_scratch, table_scratch],
        ),
        out_shape=out_type,
        compiler_params=params,
        cost_estimate=cost(1),
        name="fifth",
    )(idx, sc, blocks, l3, keep3, recv3, coef, start_block, u1, u2, u3)

    row1 = pl.BlockSpec((RB, cols, bs), lambda i, sc: (i, 0, 0))
    held = pl.BlockSpec(memory_space=pl.ANY)
    lower = pl.pallas_call(
        lower_kernel,
        grid_spec=pltpu.PrefetchScalarGridSpec(
            num_scalar_prefetch=1,
            grid=(steps_grid,),
            in_specs=[smem, pl.BlockSpec((RB, 1, cols, bs), lambda i, sc: (i, 1, 0, 0))] + [row1] * 4 + [held],
            out_specs=pl.BlockSpec((RB, 1, 2 * cols, bs), lambda i, sc: (i, 1, 0, 0)),
        ),
        out_shape=out_type,
        input_output_aliases={7: 0},
        compiler_params=params,
        name="lower",
    )(sc, coef, start_block, l1, l2, l3, l4, upper)

    own = pl.BlockSpec((HB, cols, bs), lambda i, sc: (sc[OWN_ABS], 0, 0))
    return pl.pallas_call(
        leading_kernel,
        grid_spec=pltpu.PrefetchScalarGridSpec(
            num_scalar_prefetch=1,
            grid=(1,),
            in_specs=[smem, pl.BlockSpec((HB, 1, cols, bs), lambda i, sc: (0, 1, 0, 0)), own, own, own,
                      pl.BlockSpec((HB, cols, bs), lambda i, sc: (0, 0, 0)), held],
            out_specs=pl.BlockSpec((HB, 1, 2 * cols, bs), lambda i, sc: (0, 1, 0, 0)),
        ),
        out_shape=out_type,
        input_output_aliases={7: 0},
        compiler_params=params,
        name="leading",
    )(sc, coef, start_block, keep1, keep2, keep3, keep4, lower)


def solution(mesh):
    placed = (
        P("rows", None, None, None),
        P("rows", None),
        P("rows"),
        P("rows", None, None, None),
        P("dom"),
        P("dom"),
    )
    return jax.shard_map(
        body,
        mesh=mesh,
        in_specs=placed,
        out_specs=P(("dom", "rows"), None, None, None),
        check_vma=False,
    )
```

```python
import functools

import jax
import jax.numpy as jnp
from jax import lax
from jax.experimental import pallas as pl
from jax.experimental.pallas import tpu as pltpu
from jax.sharding import PartitionSpec as P


HB = 2
RB = 8
LIMIT = 20 << 20
F32 = jnp.float32
BF16 = jnp.bfloat16


def split(value):
    high = value.astype(BF16)
    low = (value - high.astype(F32)).astype(BF16)
    return jnp.concatenate([high, low], 0)


def fold(value):
    half = value.shape[0] // 2
    return value[:half] + value[half:]


def weights(block_ref, r, m):
    return jnp.concatenate([block_ref[r, 2 * m], block_ref[r, 2 * m + 1]], 1)


def across(lhs, rhs):
    return lax.dot_general(lhs, rhs, (((1,), (1,)), ((), ())), preferred_element_type=F32)


def forward(idx_ref, read_at, block_ref, rows_ref, table_ref, r, row):
    near = [rows_ref[row]] + [rows_ref[idx_ref[row * 7 + n]] for n in range(3)]
    far = [table_ref[idx_ref[row * 7 + read_at + n]] for n in range(2)]
    total = across(jnp.concatenate(near[:2], 1), weights(block_ref, r, 0))
    total = total + across(jnp.concatenate(near[2:], 1), weights(block_ref, r, 1))
    return total + across(jnp.concatenate(far, 1), weights(block_ref, r, 2))


def scatter(idx_ref, far_at, block_ref, both, r, row, self_ref, near_ref, more_ref, part_ref):
    terms = []
    for m in range(3):
        term = fold(jnp.dot(both, weights(block_ref, r, m), preferred_element_type=F32))
        width = term.shape[1] // 2
        terms += [term[:, :width], term[:, width:]]
    self_ref[row] = terms[0]
    near_ref[idx_ref[row * 7]] += terms[1]
    near_ref[idx_ref[row * 7 + 1]] += terms[2]
    more_ref[idx_ref[row * 7 + 2]] += terms[3]
    for n in range(2):
        part_ref[idx_ref[row * 7 + far_at + n]] += terms[4 + n]


def mix(coef_ref, rows, first=0):
    out = []
    half = rows[0].shape[0] // 2
    for p in range(2):
        re = im = None
        for k, value in enumerate(rows):
            a = coef_ref[p * 10 + first + k]
            b = coef_ref[p * 10 + 5 + first + k]
            vr, vi = value[:half], value[half:]
            tr, ti = a * vr - b * vi, a * vi + b * vr
            re = tr if re is None else re + tr
            im = ti if im is None else im + ti
        out += [re, im]
    return jnp.concatenate(out, 0)


def clear(*refs):
    for ref in refs:
        ref[...] = jnp.zeros_like(ref)


def finish(sc_ref, own_at, low_ref, keep_ref, send_ref, self_ref, near_ref, more_ref, part_ref):
    half = keep_ref.shape[0]
    own = sc_ref[own_at] * HB
    for s in range(HB):
        part_ref[own + s] += self_ref[s] + near_ref[s] + more_ref[s]
    for j in range(half):
        keep_ref[j] = part_ref[j]
        send_ref[j] = part_ref[half + j].astype(BF16)
    for j in range(low_ref.shape[0]):
        low_ref[j] = self_ref[j] + near_ref[j] + more_ref[j]


def first_kernel(far_at, own_at, idx_ref, sc_ref, block_ref, drive_ref, low_ref, keep_ref, send_ref,
                 self_ref, near_ref, more_ref, part_ref):
    i = pl.program_id(0)
    count = sc_ref[0]

    @pl.when(i == 0)
    def _():
        clear(near_ref, more_ref, part_ref)

    @pl.when(i * RB < count)
    def _():
        for r in range(RB):
            row = i * RB + r
            value = jnp.where(row < count, drive_ref[r, 0], 0.0)
            scatter(idx_ref, far_at, block_ref, split(value), r, row, self_ref, near_ref, more_ref, part_ref)

    @pl.when(i * RB >= count)
    def _():
        self_ref[pl.ds(i * RB, RB)] = jnp.zeros((RB,) + self_ref.shape[1:], F32)

    @pl.when(i == pl.num_programs(0) - 1)
    def _():
        finish(sc_ref, own_at, low_ref, keep_ref, send_ref, self_ref, near_ref, more_ref, part_ref)


def fetch(local_ref, own_ref, recv_ref, rows_ref, table_ref, sem):
    half = own_ref.shape[0]
    copies = [
        pltpu.make_async_copy(own_ref, table_ref.at[pl.ds(0, half)], sem.at[0]),
        pltpu.make_async_copy(recv_ref, table_ref.at[pl.ds(half, half)], sem.at[1]),
    ]
    for copy in copies:
        copy.start()
    for j in range(rows_ref.shape[0]):
        rows_ref[j] = (local_ref[j, 0] if len(local_ref.shape) == 4 else local_ref[j]).astype(BF16)
    return copies


def patch(rows_ref, table_ref, own):
    for s in range(HB):
        rows_ref[s] = table_ref[own + s]


def middle_kernel(start, term, read_at, read_own, far_at, own_at, idx_ref, sc_ref, coef_ref, block_ref, local_ref,
                  own_ref, recv_ref, base_ref, out_ref, low_ref, keep_ref, send_ref,
                  rows_ref, table_ref, self_ref, near_ref, more_ref, part_ref, sem):
    i = pl.program_id(0)
    count = sc_ref[0]

    @pl.when(i == 0)
    def _():
        copies = fetch(local_ref, own_ref, recv_ref, rows_ref, table_ref, sem)
        clear(near_ref, more_ref, part_ref)
        for copy in copies:
            copy.wait()
        if not start:
            patch(rows_ref, table_ref, sc_ref[read_own] * HB)

    @pl.when(i * RB < count)
    def _():
        both = []
        for r in range(RB):
            row = i * RB + r
            value = forward(idx_ref, read_at, block_ref, rows_ref, table_ref, r, row)
            value = jnp.where(row < count, value, 0.0)
            both.append(split(value))
            if start:
                out_ref[r, 0] = mix(coef_ref, [base_ref[r, 0], value])
                out_ref[r, 1] = mix(coef_ref, [base_ref[r, 1]])
            else:
                out_ref[r, 0] = base_ref[r, 0] + mix(coef_ref, [value], term)
                out_ref[r, 1] = base_ref[r, 1] + mix(coef_ref, [local_ref[row]], term - 1)
        for r in range(RB):
            scatter(idx_ref, far_at, block_ref, both[r], r, i * RB + r, self_ref, near_ref, more_ref, part_ref)

    @pl.when(i * RB >= count)
    def _():
        self_ref[pl.ds(i * RB, RB)] = jnp.zeros((RB,) + self_ref.shape[1:], F32)

    @pl.when(i == pl.num_programs(0) - 1)
    def _():
        finish(sc_ref, own_at, low_ref, keep_ref, send_ref, self_ref, near_ref, more_ref, part_ref)


def last_kernel(read_at, read_own, idx_ref, sc_ref, coef_ref, block_ref, local_ref, own_ref, recv_ref, base_ref, l4_ref,
                out_ref, rows_ref, table_ref, sem):
    i = pl.program_id(0)
    count = sc_ref[0]

    @pl.when(i == 0)
    def _():
        copies = fetch(local_ref, own_ref, recv_ref, rows_ref, table_ref, sem)
        for copy in copies:
            copy.wait()
        patch(rows_ref, table_ref, sc_ref[read_own] * HB)

    @pl.when(i * RB < count)
    def _():
        for r in range(RB):
            row = i * RB + r
            alive = row < count
            value = forward(idx_ref, read_at, block_ref, rows_ref, table_ref, r, row)
            value = base_ref[r, 0] + mix(coef_ref, [value], 4)
            out_ref[r, 0] = jnp.where(alive, value, 0.0)
            lows = [local_ref[row], l4_ref[r]]
            value = base_ref[r, 1] + mix(coef_ref, lows, 3)
            out_ref[r, 1] = jnp.where(alive, value, 0.0)

    @pl.when(i * RB >= count)
    def _():
        out_ref[...] = jnp.zeros_like(out_ref)


def leading_kernel(sc_ref, coef_ref, drive_ref, k1_ref, k2_ref, k3_ref, k4_ref, held_ref, out_ref):
    for s in range(HB):
        out_ref[s, 0] = mix(coef_ref, [drive_ref[s, 0], k1_ref[s], k2_ref[s], k3_ref[s], k4_ref[s]])


def exchanges():
    def pairs(partner):
        found = []
        for i in range(32):
            c, x, y = partner(i & 1, (i >> 1) & 3, i >> 3)
            found.append((i, c | (x << 1) | (y << 3)))
        return found

    def chip(bit, first):
        def partner(c, x, y):
            if (c == 0) == first:
                return c, x ^ bit, y
            return c, x, y ^ bit
        return pairs(partner)

    core = pairs(lambda c, x, y: (c ^ 1, x, y))
    return core, [chip(1, True), chip(3, True), chip(1, False), chip(3, False)]


def body(blocks, columns, counts, start_block, shift_radius, shift_angle):
    slots, stored, bs, _ = blocks.shape
    cols = start_block.shape[2]
    owners = lax.axis_size("rows")
    table = owners * HB
    half = table // 2
    me = lax.axis_index("rows")
    core, steps = exchanges()

    owner = columns // slots
    within = columns - owner * slots
    lead = jnp.minimum(within, HB - 1)
    off = owner ^ me
    rc, rx, ry = off & 1, (off >> 1) & 3, off >> 3

    def bits(value):
        return 2 * ((value ^ (value >> 1)) & 1) + (value >> 1)

    bx, by = bits(rx), bits(ry)
    relative = 16 * rc + jnp.where((owner & 1) == 0, 4 * bx + by, 4 * by + bx)
    chip = me >> 1

    def place(device):
        gx, gy = bits((device >> 1) & 3), bits(device >> 3)
        hx, hy = bits(chip & 3) & 2, bits(chip >> 2) & 2
        return jnp.where((device & 1) == 0, 4 * (gx ^ hx) + gy, 4 * (gy ^ hy) + gx)

    absolute = 16 * rc + place(owner)
    idx = jnp.concatenate(
        [within[:, 1:4], (absolute * HB + lead)[:, 4:], (relative * HB + lead)[:, 4:]], 1
    ).reshape(-1).astype(jnp.int32)
    sc = jnp.stack([counts[0], place(me).astype(jnp.int32), jnp.int32(0), jnp.int32(0)])
    power = jnp.arange(1, 6, dtype=F32)
    size = shift_radius[:, None] ** (-power)[None]
    turn = shift_angle[:, None] * power[None]
    coef = jnp.concatenate([jnp.cos(turn) * size, -jnp.sin(turn) * size], 1).reshape(-1)

    ABS, REL = 3, 5
    OWN_ABS, OWN_REL = 1, 2
    steps_grid = slots // RB

    def live(i, sc_ref):
        return jnp.minimum(i, (sc_ref[0] - 1) // RB)

    block_spec = pl.BlockSpec((RB, stored, bs, bs), lambda i, ix, sc: (live(i, sc), 0, 0, 0))
    whole = lambda shape: pl.BlockSpec(shape, lambda i, ix, sc: (0,) * len(shape))
    row_spec = pl.BlockSpec((RB, cols, bs), lambda i, ix, sc: (i, 0, 0))
    smem = pl.BlockSpec(memory_space=pltpu.SMEM)
    acc_shape = (slots, cols, bs)
    low_shape = acc_shape
    keep_shape = (half, cols, bs)
    rows_scratch = pltpu.VMEM(acc_shape, BF16)
    table_scratch = pltpu.VMEM((table, cols, bs), BF16)
    sums = [pltpu.VMEM(acc_shape, F32)] * 3 + [pltpu.VMEM((table, cols, bs), F32)]
    sem = pltpu.SemaphoreType.DMA((2,))
    params = pltpu.CompilerParams(dimension_semantics=("arbitrary",), vmem_limit_bytes=LIMIT)
    flops = slots * stored * 2 * bs * bs * 2 * cols

    def cost(passes):
        return pl.CostEstimate(flops=passes * flops, bytes_accessed=blocks.size * 2, transcendentals=0)

    tail_shapes = [
        jax.ShapeDtypeStruct(low_shape, F32),
        jax.ShapeDtypeStruct(keep_shape, F32),
        jax.ShapeDtypeStruct(keep_shape, BF16),
    ]
    tail_specs = [whole(low_shape), whole(keep_shape), whole(keep_shape)]
    raw = pl.BlockSpec(memory_space=pl.ANY)

    def first():
        return pl.pallas_call(
            functools.partial(first_kernel, ABS, OWN_ABS),
            grid_spec=pltpu.PrefetchScalarGridSpec(
                num_scalar_prefetch=2,
                grid=(steps_grid,),
                in_specs=[block_spec, pl.BlockSpec((RB, 1, cols, bs), lambda i, ix, sc: (i, 0, 0, 0))],
                out_specs=tail_specs,
                scratch_shapes=sums,
            ),
            out_shape=tail_shapes,
            compiler_params=params,
            cost_estimate=cost(1),
            name="first",
        )(idx, sc, blocks, start_block)

    pair = pl.BlockSpec((RB, 2, 2 * cols, bs), lambda i, ix, sc: (i, 0, 0, 0))

    def middle(term, local, tables, base, read_at, read_own, far_at, own_at, name):
        start = term == 1
        local_spec = pl.BlockSpec((slots, 1, cols, bs), lambda i, ix, sc: (0, 1, 0, 0)) if start else whole(acc_shape)
        base_spec = pl.BlockSpec((RB, 2, cols, bs), lambda i, ix, sc: (i, 0, 0, 0)) if start else pair
        return pl.pallas_call(
            functools.partial(middle_kernel, start, term, read_at, read_own, far_at, own_at),
            grid_spec=pltpu.PrefetchScalarGridSpec(
                num_scalar_prefetch=2,
                grid=(steps_grid,),
                in_specs=[smem, block_spec, local_spec, raw, raw, base_spec],
                out_specs=[pair] + tail_specs,
                scratch_shapes=[rows_scratch, table_scratch] + sums + [sem],
            ),
            out_shape=[out_type] + tail_shapes,
            compiler_params=params,
            cost_estimate=cost(2),
            name=name,
        )(idx, sc, coef, blocks, local, *tables, base)

    out_type = jax.ShapeDtypeStruct((slots, 2, 2 * cols, bs), F32)

    def last(local, tables, base, low):
        return pl.pallas_call(
            functools.partial(last_kernel, ABS, OWN_ABS),
            grid_spec=pltpu.PrefetchScalarGridSpec(
                num_scalar_prefetch=2,
                grid=(steps_grid,),
                in_specs=[smem, block_spec, whole(acc_shape), raw, raw, pair, row_spec],
                out_specs=pair,
                scratch_shapes=[rows_scratch, table_scratch, sem],
            ),
            out_shape=out_type,
            compiler_params=params,
            cost_estimate=cost(1),
            name="fifth",
        )(idx, sc, coef, blocks, local, *tables, base, low)

    def leading(keeps, done):
        own = pl.BlockSpec((HB, cols, bs), lambda i, sc: (sc[OWN_ABS], 0, 0))
        return pl.pallas_call(
            leading_kernel,
            grid_spec=pltpu.PrefetchScalarGridSpec(
                num_scalar_prefetch=1,
                grid=(1,),
                in_specs=[smem, pl.BlockSpec((HB, 1, cols, bs), lambda i, sc: (0, 1, 0, 0)), own, own, own,
                          pl.BlockSpec((HB, cols, bs), lambda i, sc: (0, 0, 0)), raw],
                out_specs=pl.BlockSpec((HB, 1, 2 * cols, bs), lambda i, sc: (0, 1, 0, 0)),
            ),
            out_shape=out_type,
            input_output_aliases={7: 0},
            compiler_params=params,
            name="leading",
        )(sc, coef, start_block, *keeps, done)

    def send(value, step):
        return lax.ppermute(value, "rows", step)

    def narrow(value):
        return value.astype(BF16)

    def join(value, more):
        return jnp.concatenate([value, more], 0)

    ma, mb, mc, md = steps
    part = half // 2

    def everywhere(value, sent):
        value = value + send(sent, core)
        value = value[:part] + send(narrow(value[part:]), ma)
        for step in (mb, mc, md):
            value = value + send(narrow(value), step)
        mine = narrow(value)
        mine = join(mine, send(mine, ma))
        return value, (mine, send(mine, core))

    h = narrow(start_block[:HB, 1])
    for step in (md, mc, mb, ma):
        h = join(h, send(h, step))
    h = (h, send(h, core))
    l1, a, sent = first()
    a, ta = everywhere(a, sent)
    base, l2, b, sent = middle(1, start_block, h, start_block, REL, OWN_REL, ABS, OWN_ABS, "second")
    b, tb = everywhere(b, sent)
    base, l3, c, sent = middle(2, l1, ta, base, ABS, OWN_ABS, ABS, OWN_ABS, "third")
    c, tc = everywhere(c, sent)
    base, l4, d, sent = middle(3, l2, tb, base, ABS, OWN_ABS, REL, OWN_REL, "fourth")
    d = d + send(sent, core)
    for step in steps:
        size = d.shape[0] // 2
        d = d[:size] + send(narrow(d[size:]), step)
    done = last(l3, tc, base, l4)
    return leading((a, b, c, d), done)


def solution(mesh):
    placed = (
        P("rows", None, None, None),
        P("rows", None),
        P("rows"),
        P("rows", None, None, None),
        P("dom"),
        P("dom"),
    )
    return jax.shard_map(
        body,
        mesh=mesh,
        in_specs=placed,
        out_specs=P(("dom", "rows"), None, None, None),
        check_vma=False,
    )
```

```python
import functools

import jax
import jax.numpy as jnp
from jax import lax
from jax.experimental import pallas as pl
from jax.experimental.pallas import tpu as pltpu
from jax.sharding import PartitionSpec as P


HB = 2
RB = 8
LIMIT = 20 << 20
F32 = jnp.float32
BF16 = jnp.bfloat16


def split(value):
    high = value.astype(BF16)
    low = (value - high.astype(F32)).astype(BF16)
    return jnp.concatenate([high, low], 0)


def fold(value):
    half = value.shape[0] // 2
    return value[:half] + value[half:]


def weights(block_ref, r, m):
    return jnp.concatenate([block_ref[r, 2 * m], block_ref[r, 2 * m + 1]], 1)


def across(lhs, rhs):
    return lax.dot_general(lhs, rhs, (((1,), (1,)), ((), ())), preferred_element_type=F32)


def forward(idx_ref, read_at, block_ref, rows_ref, table_ref, r, row):
    near = [rows_ref[row]] + [rows_ref[idx_ref[row * 9 + n]] for n in range(3)]
    far = [table_ref[idx_ref[row * 9 + read_at + n]] for n in range(2)]
    total = across(jnp.concatenate(near[:2], 1), weights(block_ref, r, 0))
    total = total + across(jnp.concatenate(near[2:], 1), weights(block_ref, r, 1))
    return total + across(jnp.concatenate(far, 1), weights(block_ref, r, 2))


def scatter(idx_ref, far_at, block_ref, both, r, row, self_ref, near_ref, more_ref, part_ref):
    terms = []
    for m in range(3):
        term = fold(jnp.dot(both, weights(block_ref, r, m), preferred_element_type=F32))
        width = term.shape[1] // 2
        terms += [term[:, :width], term[:, width:]]
    self_ref[row] = terms[0]
    near_ref[idx_ref[row * 9]] += terms[1]
    near_ref[idx_ref[row * 9 + 1]] += terms[2]
    more_ref[idx_ref[row * 9 + 2]] += terms[3]
    for n in range(2):
        part_ref[idx_ref[row * 9 + far_at + n]] += terms[4 + n]


def mix(coef_ref, rows, first=0):
    out = []
    half = rows[0].shape[0] // 2
    for p in range(2):
        re = im = None
        for k, value in enumerate(rows):
            a = coef_ref[p * 10 + first + k]
            b = coef_ref[p * 10 + 5 + first + k]
            vr, vi = value[:half], value[half:]
            tr, ti = a * vr - b * vi, a * vi + b * vr
            re = tr if re is None else re + tr
            im = ti if im is None else im + ti
        out += [re, im]
    return jnp.concatenate(out, 0)


def clear(*refs):
    for ref in refs:
        ref[...] = jnp.zeros_like(ref)


def finish(sc_ref, own_at, low_ref, keep_ref, send_ref, self_ref, near_ref, more_ref, part_ref):
    half = keep_ref.shape[0]
    own = sc_ref[own_at] * HB
    for s in range(HB):
        part_ref[own + s] += self_ref[s] + near_ref[s] + more_ref[s]
    for j in range(half):
        keep_ref[j] = part_ref[j]
        send_ref[j] = part_ref[half + j].astype(BF16)
    for j in range(low_ref.shape[0]):
        low_ref[j] = self_ref[j] + near_ref[j] + more_ref[j]


def first_kernel(far_at, own_at, idx_ref, sc_ref, block_ref, drive_ref, low_ref, keep_ref, send_ref,
                 self_ref, near_ref, more_ref, part_ref):
    i = pl.program_id(0)
    count = sc_ref[0]

    @pl.when(i == 0)
    def _():
        clear(near_ref, more_ref, part_ref)

    @pl.when(i * RB < count)
    def _():
        for r in range(RB):
            row = i * RB + r
            value = jnp.where(row < count, drive_ref[r, 0], 0.0)
            scatter(idx_ref, far_at, block_ref, split(value), r, row, self_ref, near_ref, more_ref, part_ref)

    @pl.when(i * RB >= count)
    def _():
        self_ref[pl.ds(i * RB, RB)] = jnp.zeros((RB,) + self_ref.shape[1:], F32)

    @pl.when(i == pl.num_programs(0) - 1)
    def _():
        finish(sc_ref, own_at, low_ref, keep_ref, send_ref, self_ref, near_ref, more_ref, part_ref)


def fetch(local_ref, own_ref, recv_ref, rows_ref, table_ref, sem):
    half = own_ref.shape[0]
    if half == table_ref.shape[0]:
        copies = [pltpu.make_async_copy(own_ref, table_ref, sem.at[0])]
    else:
        copies = [
            pltpu.make_async_copy(own_ref, table_ref.at[pl.ds(0, half)], sem.at[0]),
            pltpu.make_async_copy(recv_ref, table_ref.at[pl.ds(half, half)], sem.at[1]),
        ]
    for copy in copies:
        copy.start()
    for j in range(rows_ref.shape[0]):
        rows_ref[j] = (local_ref[j, 0] if len(local_ref.shape) == 4 else local_ref[j]).astype(BF16)
    return copies


def patch(rows_ref, table_ref, own):
    for s in range(HB):
        rows_ref[s] = table_ref[own + s]


def middle_kernel(start, term, read_at, read_own, far_at, own_at, idx_ref, sc_ref, coef_ref, block_ref, local_ref,
                  own_ref, recv_ref, base_ref, out_ref, low_ref, keep_ref, send_ref,
                  rows_ref, table_ref, self_ref, near_ref, more_ref, part_ref, sem):
    i = pl.program_id(0)
    count = sc_ref[0]

    @pl.when(i == 0)
    def _():
        copies = fetch(local_ref, own_ref, recv_ref, rows_ref, table_ref, sem)
        clear(near_ref, more_ref, part_ref)
        for copy in copies:
            copy.wait()
        if not start:
            patch(rows_ref, table_ref, sc_ref[read_own] * HB)

    @pl.when(i * RB < count)
    def _():
        both = []
        for r in range(RB):
            row = i * RB + r
            value = forward(idx_ref, read_at, block_ref, rows_ref, table_ref, r, row)
            value = jnp.where(row < count, value, 0.0)
            both.append(split(value))
            if start:
                out_ref[r, 0] = mix(coef_ref, [base_ref[r, 0], value])
                out_ref[r, 1] = mix(coef_ref, [base_ref[r, 1]])
            else:
                out_ref[r, 0] = base_ref[r, 0] + mix(coef_ref, [value], term)
                out_ref[r, 1] = base_ref[r, 1] + mix(coef_ref, [local_ref[row]], term - 1)
        for r in range(RB):
            scatter(idx_ref, far_at, block_ref, both[r], r, i * RB + r, self_ref, near_ref, more_ref, part_ref)

    @pl.when(i * RB >= count)
    def _():
        self_ref[pl.ds(i * RB, RB)] = jnp.zeros((RB,) + self_ref.shape[1:], F32)

    @pl.when(i == pl.num_programs(0) - 1)
    def _():
        finish(sc_ref, own_at, low_ref, keep_ref, send_ref, self_ref, near_ref, more_ref, part_ref)


def last_kernel(read_at, read_own, idx_ref, sc_ref, coef_ref, block_ref, local_ref, own_ref, recv_ref, base_ref, l4_ref,
                drive_ref, k1_ref, k2_ref, k3_ref, k4_ref, out_hbm, rows_ref, table_ref, full_ref, sem, out_sem):
    i = pl.program_id(0)
    count = sc_ref[0]

    def store(j):
        at = pl.ds(pl.multiple_of(j * RB, RB), RB)
        return pltpu.make_async_copy(full_ref.at[at], out_hbm.at[at], out_sem.at[j])

    @pl.when(i == 0)
    def _():
        copies = fetch(local_ref, own_ref, recv_ref, rows_ref, table_ref, sem)
        for copy in copies:
            copy.wait()
        patch(rows_ref, table_ref, sc_ref[read_own] * HB)

    @pl.when(i * RB < count)
    def _():
        for r in range(RB):
            row = i * RB + r
            alive = row < count
            value = forward(idx_ref, read_at, block_ref, rows_ref, table_ref, r, row)
            value = base_ref[r, 0] + mix(coef_ref, [value], 4)
            full_ref[row, 0] = jnp.where(alive, value, 0.0)
            value = base_ref[r, 1] + mix(coef_ref, [local_ref[row], l4_ref[r]], 3)
            full_ref[row, 1] = jnp.where(alive, value, 0.0)

    @pl.when(i * RB >= count)
    def _():
        full_ref[pl.ds(i * RB, RB)] = jnp.zeros((RB,) + full_ref.shape[1:], F32)

    @pl.when(i == 0)
    def _():
        for s in range(HB):
            full_ref[s, 1] = mix(coef_ref, [drive_ref[s, 0], k1_ref[s], k2_ref[s], k3_ref[s], k4_ref[s]])

    store(i).start()

    @pl.when(i == pl.num_programs(0) - 1)
    def _():
        for j in range(full_ref.shape[0] // RB):
            store(j).wait()


def exchanges():
    def pairs(partner):
        found = []
        for i in range(32):
            c, x, y = partner(i & 1, (i >> 1) & 3, i >> 3)
            found.append((i, c | (x << 1) | (y << 3)))
        return found

    def chip(bit, first):
        def partner(c, x, y):
            if (c == 0) == first:
                return c, x ^ bit, y
            return c, x, y ^ bit

        return pairs(partner)

    core = pairs(lambda c, x, y: (c ^ 1, x, y))
    return core, [chip(1, True), chip(3, True), chip(1, False), chip(3, False)]


def body(blocks, columns, counts, start_block, shift_radius, shift_angle):
    slots, stored, bs, _ = blocks.shape
    cols = start_block.shape[2]
    owners = lax.axis_size("rows")
    table = owners * HB
    half = table // 2
    me = lax.axis_index("rows")
    core, steps = exchanges()

    owner = columns // slots
    within = columns - owner * slots
    lead = jnp.minimum(within, HB - 1)
    off = owner ^ me
    rc, rx, ry = off & 1, (off >> 1) & 3, off >> 3

    def bits(value):
        return 2 * ((value ^ (value >> 1)) & 1) + (value >> 1)

    bx, by = bits(rx), bits(ry)
    relative = 16 * rc + jnp.where((owner & 1) == 0, 4 * bx + by, 4 * by + bx)
    chip = me >> 1

    def place(device):
        gx, gy = bits((device >> 1) & 3), bits(device >> 3)
        hx, hy = bits(chip & 3) & 2, bits(chip >> 2) & 2
        return jnp.where((device & 1) == 0, 4 * (gx ^ hx) + gy, 4 * (gy ^ hy) + gx)

    absolute = 16 * rc + place(owner)
    idx = jnp.concatenate(
        [within[:, 1:4]] + [(where * HB + lead)[:, 4:] for where in (absolute, relative, owner)], 1
    ).reshape(-1).astype(jnp.int32)
    sc = jnp.stack([counts[0], place(me).astype(jnp.int32), jnp.int32(0), jnp.int32(0)])
    power = jnp.arange(1, 6, dtype=F32)
    size = shift_radius[:, None] ** (-power)[None]
    turn = shift_angle[:, None] * power[None]
    coef = jnp.concatenate([jnp.cos(turn) * size, -jnp.sin(turn) * size], 1).reshape(-1)

    ABS, REL, OWNER = 3, 5, 7
    OWN_ABS, OWN_REL = 1, 2
    steps_grid = slots // RB

    def live(i, sc_ref):
        return jnp.minimum(i, (sc_ref[0] - 1) // RB)

    block_spec = pl.BlockSpec((RB, stored, bs, bs), lambda i, ix, sc: (live(i, sc), 0, 0, 0))
    whole = lambda shape: pl.BlockSpec(shape, lambda i, ix, sc: (0,) * len(shape))
    row_spec = pl.BlockSpec((RB, cols, bs), lambda i, ix, sc: (i, 0, 0))
    smem = pl.BlockSpec(memory_space=pltpu.SMEM)
    acc_shape = (slots, cols, bs)
    low_shape = acc_shape
    keep_shape = (half, cols, bs)
    rows_scratch = pltpu.VMEM(acc_shape, BF16)
    table_scratch = pltpu.VMEM((table, cols, bs), BF16)
    sums = [pltpu.VMEM(acc_shape, F32)] * 3 + [pltpu.VMEM((table, cols, bs), F32)]
    sem = pltpu.SemaphoreType.DMA((2,))
    params = pltpu.CompilerParams(dimension_semantics=("arbitrary",), vmem_limit_bytes=LIMIT)
    flops = slots * stored * 2 * bs * bs * 2 * cols

    def cost(passes):
        return pl.CostEstimate(flops=passes * flops, bytes_accessed=blocks.size * 2, transcendentals=0)

    tail_shapes = [
        jax.ShapeDtypeStruct(low_shape, F32),
        jax.ShapeDtypeStruct(keep_shape, F32),
        jax.ShapeDtypeStruct(keep_shape, BF16),
    ]
    tail_specs = [whole(low_shape), whole(keep_shape), whole(keep_shape)]
    raw = pl.BlockSpec(memory_space=pl.ANY)

    def first():
        return pl.pallas_call(
            functools.partial(first_kernel, ABS, OWN_ABS),
            grid_spec=pltpu.PrefetchScalarGridSpec(
                num_scalar_prefetch=2,
                grid=(steps_grid,),
                in_specs=[block_spec, pl.BlockSpec((RB, 1, cols, bs), lambda i, ix, sc: (i, 0, 0, 0))],
                out_specs=tail_specs,
                scratch_shapes=sums,
            ),
            out_shape=tail_shapes,
            compiler_params=params,
            cost_estimate=cost(1),
            name="first",
        )(idx, sc, blocks, start_block)

    pair = pl.BlockSpec((RB, 2, 2 * cols, bs), lambda i, ix, sc: (i, 0, 0, 0))

    def middle(term, local, tables, base, read_at, read_own, far_at, own_at):
        start = term == 1
        local_spec = pl.BlockSpec((slots, 1, cols, bs), lambda i, ix, sc: (0, 1, 0, 0)) if start else whole(acc_shape)
        base_spec = pl.BlockSpec((RB, 2, cols, bs), lambda i, ix, sc: (i, 0, 0, 0)) if start else pair
        return pl.pallas_call(
            functools.partial(middle_kernel, start, term, read_at, read_own, far_at, own_at),
            grid_spec=pltpu.PrefetchScalarGridSpec(
                num_scalar_prefetch=2,
                grid=(steps_grid,),
                in_specs=[smem, block_spec, local_spec, raw, raw, base_spec],
                out_specs=[pair] + tail_specs,
                scratch_shapes=[rows_scratch, table_scratch] + sums + [sem],
            ),
            out_shape=[out_type] + tail_shapes,
            compiler_params=params,
            cost_estimate=cost(2),
        )(idx, sc, coef, blocks, local, *tables, base)

    out_type = jax.ShapeDtypeStruct((slots, 2, 2 * cols, bs), F32)

    def last(local, tables, base, low, keeps):
        own = pl.BlockSpec((HB, cols, bs), lambda i, ix, sc: (sc[OWN_ABS], 0, 0))
        return pl.pallas_call(
            functools.partial(last_kernel, ABS, OWN_ABS),
            grid_spec=pltpu.PrefetchScalarGridSpec(
                num_scalar_prefetch=2,
                grid=(steps_grid,),
                in_specs=[smem, block_spec, whole(acc_shape), raw, raw, pair, row_spec,
                          pl.BlockSpec((HB, 1, cols, bs), lambda i, ix, sc: (0, 1, 0, 0)), own, own, own,
                          pl.BlockSpec((HB, cols, bs), lambda i, ix, sc: (0, 0, 0))],
                out_specs=raw,
                scratch_shapes=[rows_scratch, table_scratch, pltpu.VMEM((slots, 2, 2 * cols, bs), F32), sem,
                                pltpu.SemaphoreType.DMA((steps_grid,))],
            ),
            out_shape=out_type,
            compiler_params=params,
            cost_estimate=cost(1),
            name="fifth",
        )(idx, sc, coef, blocks, local, *tables, base, low, start_block, *keeps)

    def send(value, step):
        return lax.ppermute(value, "rows", step)

    def narrow(value):
        return value.astype(BF16)

    def join(value, more):
        return jnp.concatenate([value, more], 0)

    ma, mb, mc, md = steps
    part = half // 2

    def around(value, left):
        for step in left:
            value = value + send(narrow(value), step)
        mine = narrow(value)
        mine = join(mine, send(mine, ma))
        return value, (mine, send(mine, core))

    def everywhere(value, sent):
        value = value + send(sent, core)
        value = value[:part] + send(narrow(value[part:]), ma)
        return around(value, (mb, mc, md))

    h = narrow(start_block[:HB, 1])
    h = jnp.broadcast_to(h[None], (owners,) + h.shape)
    h = lax.all_to_all(h, "rows", 0, 0, tiled=True)
    l1, a, sent = first()
    h = h.reshape((table,) + h.shape[2:])
    a = a + send(sent, core)
    sent, h = lax.optimization_barrier((narrow(a[part:]), h))
    a = a[:part] + send(sent, ma)
    more, ta = around(a, (mb, mc, md))
    base, l2, b, sent = middle(1, start_block, (h, h), start_block, OWNER, OWN_REL, ABS, OWN_ABS)
    a = more
    b, tb = everywhere(b, sent)
    base, l3, c, sent = middle(2, l1, ta, base, ABS, OWN_ABS, ABS, OWN_ABS)
    c, tc = everywhere(c, sent)
    base, l4, d, sent = middle(3, l2, tb, base, ABS, OWN_ABS, REL, OWN_REL)
    d = d + send(sent, core)
    for step in steps:
        size = d.shape[0] // 2
        d = d[:size] + send(narrow(d[size:]), step)
    return last(l3, tc, base, l4, (a, b, c, d))


def solution(mesh):
    placed = (
        P("rows", None, None, None),
        P("rows", None),
        P("rows"),
        P("rows", None, None, None),
        P("dom"),
        P("dom"),
    )
    return jax.shard_map(
        body,
        mesh=mesh,
        in_specs=placed,
        out_specs=P(("dom", "rows"), None, None, None),
        check_vma=False,
    )
```

```python
import functools

import jax
import jax.numpy as jnp
from jax import lax
from jax.experimental import pallas as pl
from jax.experimental.pallas import tpu as pltpu
from jax.sharding import PartitionSpec as P


HB = 2
RB = 8
LIMIT = 20 << 20
F32 = jnp.float32
BF16 = jnp.bfloat16


def split(value):
    high = value.astype(BF16)
    low = (value - high.astype(F32)).astype(BF16)
    return jnp.concatenate([high, low], 0)


def fold(value):
    half = value.shape[0] // 2
    return value[:half] + value[half:]


def weights(block_ref, r, m):
    return jnp.concatenate([block_ref[r, 2 * m], block_ref[r, 2 * m + 1]], 1)


def across(lhs, rhs):
    return lax.dot_general(lhs, rhs, (((1,), (1,)), ((), ())), preferred_element_type=F32)


def forward(idx_ref, read_at, block_ref, rows_ref, table_ref, r, row):
    near = [rows_ref[row]] + [rows_ref[idx_ref[row * 7 + n]] for n in range(3)]
    far = [table_ref[idx_ref[row * 7 + read_at + n]] for n in range(2)]
    total = across(jnp.concatenate(near[:2], 1), weights(block_ref, r, 0))
    total = total + across(jnp.concatenate(near[2:], 1), weights(block_ref, r, 1))
    return total + across(jnp.concatenate(far, 1), weights(block_ref, r, 2))


def scatter(idx_ref, far_at, block_ref, both, r, row, self_ref, near_ref, more_ref, part_ref):
    terms = []
    for m in range(3):
        term = fold(jnp.dot(both, weights(block_ref, r, m), preferred_element_type=F32))
        width = term.shape[1] // 2
        terms += [term[:, :width], term[:, width:]]
    self_ref[row] = terms[0]
    near_ref[idx_ref[row * 7]] += terms[1]
    near_ref[idx_ref[row * 7 + 1]] += terms[2]
    more_ref[idx_ref[row * 7 + 2]] += terms[3]
    for n in range(2):
        part_ref[idx_ref[row * 7 + far_at + n]] += terms[4 + n]


def mix(coef_ref, rows, first=0):
    out = []
    half = rows[0].shape[0] // 2
    for p in range(2):
        re = im = None
        for k, value in enumerate(rows):
            a = coef_ref[p * 10 + first + k]
            b = coef_ref[p * 10 + 5 + first + k]
            vr, vi = value[:half], value[half:]
            tr, ti = a * vr - b * vi, a * vi + b * vr
            re = tr if re is None else re + tr
            im = ti if im is None else im + ti
        out += [re, im]
    return jnp.concatenate(out, 0)


def clear(*refs):
    for ref in refs:
        ref[...] = jnp.zeros_like(ref)


def finish(sc_ref, own_at, low_ref, keep_ref, send_ref, self_ref, near_ref, more_ref, part_ref):
    half = keep_ref.shape[0]
    own = sc_ref[own_at] * HB
    for s in range(HB):
        part_ref[own + s] += self_ref[s] + near_ref[s] + more_ref[s]
    for j in range(half):
        keep_ref[j] = part_ref[j]
        send_ref[j] = part_ref[half + j].astype(BF16)
    for j in range(low_ref.shape[0]):
        low_ref[j] = self_ref[j] + near_ref[j] + more_ref[j]


def first_kernel(far_at, own_at, idx_ref, sc_ref, block_ref, drive_ref, low_ref, keep_ref, send_ref,
                 self_ref, near_ref, more_ref, part_ref):
    i = pl.program_id(0)
    count = sc_ref[0]

    @pl.when(i == 0)
    def _():
        clear(near_ref, more_ref, part_ref)

    @pl.when(i * RB < count)
    def _():
        for r in range(RB):
            row = i * RB + r
            value = jnp.where(row < count, drive_ref[r, 0], 0.0)
            scatter(idx_ref, far_at, block_ref, split(value), r, row, self_ref, near_ref, more_ref, part_ref)

    @pl.when(i * RB >= count)
    def _():
        self_ref[pl.ds(i * RB, RB)] = jnp.zeros((RB,) + self_ref.shape[1:], F32)

    @pl.when(i == pl.num_programs(0) - 1)
    def _():
        finish(sc_ref, own_at, low_ref, keep_ref, send_ref, self_ref, near_ref, more_ref, part_ref)


def fetch(local_ref, own_ref, recv_ref, rows_ref, table_ref, sem):
    half = own_ref.shape[0]
    copies = [
        pltpu.make_async_copy(own_ref, table_ref.at[pl.ds(0, half)], sem.at[0]),
        pltpu.make_async_copy(recv_ref, table_ref.at[pl.ds(half, half)], sem.at[1]),
    ]
    for copy in copies:
        copy.start()
    for j in range(rows_ref.shape[0]):
        rows_ref[j] = (local_ref[j, 0] if len(local_ref.shape) == 4 else local_ref[j]).astype(BF16)
    return copies


def patch(rows_ref, table_ref, own):
    for s in range(HB):
        rows_ref[s] = table_ref[own + s]


def middle_kernel(start, term, read_at, read_own, far_at, own_at, idx_ref, sc_ref, coef_ref, block_ref, local_ref,
                  own_ref, recv_ref, base_ref, out_ref, low_ref, keep_ref, send_ref,
                  rows_ref, table_ref, self_ref, near_ref, more_ref, part_ref, sem):
    i = pl.program_id(0)
    count = sc_ref[0]

    @pl.when(i == 0)
    def _():
        copies = fetch(local_ref, own_ref, recv_ref, rows_ref, table_ref, sem)
        clear(near_ref, more_ref, part_ref)
        for copy in copies:
            copy.wait()
        if not start:
            patch(rows_ref, table_ref, sc_ref[read_own] * HB)

    @pl.when(i * RB < count)
    def _():
        both = []
        for r in range(RB):
            row = i * RB + r
            value = forward(idx_ref, read_at, block_ref, rows_ref, table_ref, r, row)
            value = jnp.where(row < count, value, 0.0)
            both.append(split(value))
            if start:
                out_ref[r, 0] = mix(coef_ref, [base_ref[r, 0], value])
                out_ref[r, 1] = mix(coef_ref, [base_ref[r, 1]])
            else:
                out_ref[r, 0] = base_ref[r, 0] + mix(coef_ref, [value], term)
                out_ref[r, 1] = base_ref[r, 1] + mix(coef_ref, [local_ref[row]], term - 1)
        for r in range(RB):
            scatter(idx_ref, far_at, block_ref, both[r], r, i * RB + r, self_ref, near_ref, more_ref, part_ref)

    @pl.when(i * RB >= count)
    def _():
        self_ref[pl.ds(i * RB, RB)] = jnp.zeros((RB,) + self_ref.shape[1:], F32)

    @pl.when(i == pl.num_programs(0) - 1)
    def _():
        finish(sc_ref, own_at, low_ref, keep_ref, send_ref, self_ref, near_ref, more_ref, part_ref)


def last_kernel(read_at, read_own, idx_ref, sc_ref, coef_ref, block_ref, local_ref, own_ref, recv_ref, base_ref, l4_ref,
                drive_ref, k1_ref, k2_ref, k3_ref, k4_ref, out_hbm, rows_ref, table_ref, full_ref, sem, out_sem):
    i = pl.program_id(0)
    count = sc_ref[0]

    def store(j):
        at = pl.ds(pl.multiple_of(j * RB, RB), RB)
        return pltpu.make_async_copy(full_ref.at[at], out_hbm.at[at], out_sem.at[j])

    @pl.when(i == 0)
    def _():
        copies = fetch(local_ref, own_ref, recv_ref, rows_ref, table_ref, sem)
        for copy in copies:
            copy.wait()
        patch(rows_ref, table_ref, sc_ref[read_own] * HB)

    @pl.when(i * RB < count)
    def _():
        for r in range(RB):
            row = i * RB + r
            alive = row < count
            value = forward(idx_ref, read_at, block_ref, rows_ref, table_ref, r, row)
            value = base_ref[r, 0] + mix(coef_ref, [value], 4)
            full_ref[row, 0] = jnp.where(alive, value, 0.0)
            value = base_ref[r, 1] + mix(coef_ref, [local_ref[row], l4_ref[r]], 3)
            full_ref[row, 1] = jnp.where(alive, value, 0.0)

    @pl.when(i * RB >= count)
    def _():
        full_ref[pl.ds(i * RB, RB)] = jnp.zeros((RB,) + full_ref.shape[1:], F32)

    @pl.when(i == 0)
    def _():
        for s in range(HB):
            full_ref[s, 1] = mix(coef_ref, [drive_ref[s, 0], k1_ref[s], k2_ref[s], k3_ref[s], k4_ref[s]])

    store(i).start()

    @pl.when(i == pl.num_programs(0) - 1)
    def _():
        for j in range(full_ref.shape[0] // RB):
            store(j).wait()


def exchanges():
    def pairs(partner):
        found = []
        for i in range(32):
            c, x, y = partner(i & 1, (i >> 1) & 3, i >> 3)
            found.append((i, c | (x << 1) | (y << 3)))
        return found

    def chip(bit, first):
        def partner(c, x, y):
            if (c == 0) == first:
                return c, x ^ bit, y
            return c, x, y ^ bit
        return pairs(partner)

    core = pairs(lambda c, x, y: (c ^ 1, x, y))
    return core, [chip(1, True), chip(3, True), chip(1, False), chip(3, False)]


def body(blocks, columns, counts, start_block, shift_radius, shift_angle):
    slots, stored, bs, _ = blocks.shape
    cols = start_block.shape[2]
    owners = lax.axis_size("rows")
    table = owners * HB
    half = table // 2
    me = lax.axis_index("rows")
    core, steps = exchanges()

    owner = columns // slots
    within = columns - owner * slots
    lead = jnp.minimum(within, HB - 1)
    off = owner ^ me
    rc, rx, ry = off & 1, (off >> 1) & 3, off >> 3

    def bits(value):
        return 2 * ((value ^ (value >> 1)) & 1) + (value >> 1)

    bx, by = bits(rx), bits(ry)
    relative = 16 * rc + jnp.where((owner & 1) == 0, 4 * bx + by, 4 * by + bx)
    chip = me >> 1

    def place(device):
        gx, gy = bits((device >> 1) & 3), bits(device >> 3)
        hx, hy = bits(chip & 3) & 2, bits(chip >> 2) & 2
        return jnp.where((device & 1) == 0, 4 * (gx ^ hx) + gy, 4 * (gy ^ hy) + gx)

    absolute = 16 * rc + place(owner)
    idx = jnp.concatenate(
        [within[:, 1:4], (absolute * HB + lead)[:, 4:], (relative * HB + lead)[:, 4:]], 1
    ).reshape(-1).astype(jnp.int32)
    sc = jnp.stack([counts[0], place(me).astype(jnp.int32), jnp.int32(0), jnp.int32(0)])
    power = jnp.arange(1, 6, dtype=F32)
    size = shift_radius[:, None] ** (-power)[None]
    turn = shift_angle[:, None] * power[None]
    coef = jnp.concatenate([jnp.cos(turn) * size, -jnp.sin(turn) * size], 1).reshape(-1)

    ABS, REL = 3, 5
    OWN_ABS, OWN_REL = 1, 2
    steps_grid = slots // RB

    def live(i, sc_ref):
        return jnp.minimum(i, (sc_ref[0] - 1) // RB)

    block_spec = pl.BlockSpec((RB, stored, bs, bs), lambda i, ix, sc: (live(i, sc), 0, 0, 0))
    whole = lambda shape: pl.BlockSpec(shape, lambda i, ix, sc: (0,) * len(shape))
    row_spec = pl.BlockSpec((RB, cols, bs), lambda i, ix, sc: (i, 0, 0))
    smem = pl.BlockSpec(memory_space=pltpu.SMEM)
    acc_shape = (slots, cols, bs)
    low_shape = acc_shape
    keep_shape = (half, cols, bs)
    rows_scratch = pltpu.VMEM(acc_shape, BF16)
    table_scratch = pltpu.VMEM((table, cols, bs), BF16)
    sums = [pltpu.VMEM(acc_shape, F32)] * 3 + [pltpu.VMEM((table, cols, bs), F32)]
    sem = pltpu.SemaphoreType.DMA((2,))
    params = pltpu.CompilerParams(dimension_semantics=("arbitrary",), vmem_limit_bytes=LIMIT)
    flops = slots * stored * 2 * bs * bs * 2 * cols

    def cost(passes):
        return pl.CostEstimate(flops=passes * flops, bytes_accessed=blocks.size * 2, transcendentals=0)

    tail_shapes = [
        jax.ShapeDtypeStruct(low_shape, F32),
        jax.ShapeDtypeStruct(keep_shape, F32),
        jax.ShapeDtypeStruct(keep_shape, BF16),
    ]
    tail_specs = [whole(low_shape), whole(keep_shape), whole(keep_shape)]
    raw = pl.BlockSpec(memory_space=pl.ANY)

    def first():
        return pl.pallas_call(
            functools.partial(first_kernel, ABS, OWN_ABS),
            grid_spec=pltpu.PrefetchScalarGridSpec(
                num_scalar_prefetch=2,
                grid=(steps_grid,),
                in_specs=[block_spec, pl.BlockSpec((RB, 1, cols, bs), lambda i, ix, sc: (i, 0, 0, 0))],
                out_specs=tail_specs,
                scratch_shapes=sums,
            ),
            out_shape=tail_shapes,
            compiler_params=params,
            cost_estimate=cost(1),
            name="first",
        )(idx, sc, blocks, start_block)

    pair = pl.BlockSpec((RB, 2, 2 * cols, bs), lambda i, ix, sc: (i, 0, 0, 0))

    def middle(term, local, tables, base, read_at, read_own, far_at, own_at, name):
        start = term == 1
        local_spec = pl.BlockSpec((slots, 1, cols, bs), lambda i, ix, sc: (0, 1, 0, 0)) if start else whole(acc_shape)
        base_spec = pl.BlockSpec((RB, 2, cols, bs), lambda i, ix, sc: (i, 0, 0, 0)) if start else pair
        return pl.pallas_call(
            functools.partial(middle_kernel, start, term, read_at, read_own, far_at, own_at),
            grid_spec=pltpu.PrefetchScalarGridSpec(
                num_scalar_prefetch=2,
                grid=(steps_grid,),
                in_specs=[smem, block_spec, local_spec, raw, raw, base_spec],
                out_specs=[pair] + tail_specs,
                scratch_shapes=[rows_scratch, table_scratch] + sums + [sem],
            ),
            out_shape=[out_type] + tail_shapes,
            compiler_params=params,
            cost_estimate=cost(2),
            name=name,
        )(idx, sc, coef, blocks, local, *tables, base)

    out_type = jax.ShapeDtypeStruct((slots, 2, 2 * cols, bs), F32)

    def last(local, tables, base, low, keeps):
        own = pl.BlockSpec((HB, cols, bs), lambda i, ix, sc: (sc[OWN_ABS], 0, 0))
        return pl.pallas_call(
            functools.partial(last_kernel, ABS, OWN_ABS),
            grid_spec=pltpu.PrefetchScalarGridSpec(
                num_scalar_prefetch=2,
                grid=(steps_grid,),
                in_specs=[smem, block_spec, whole(acc_shape), raw, raw, pair, row_spec,
                          pl.BlockSpec((HB, 1, cols, bs), lambda i, ix, sc: (0, 1, 0, 0)), own, own, own,
                          pl.BlockSpec((HB, cols, bs), lambda i, ix, sc: (0, 0, 0))],
                out_specs=raw,
                scratch_shapes=[rows_scratch, table_scratch, pltpu.VMEM((slots, 2, 2 * cols, bs), F32), sem,
                                pltpu.SemaphoreType.DMA((steps_grid,))],
            ),
            out_shape=out_type,
            compiler_params=params,
            cost_estimate=cost(1),
            name="fifth",
        )(idx, sc, coef, blocks, local, *tables, base, low, start_block, *keeps)

    def send(value, step):
        return lax.ppermute(value, "rows", step)

    def narrow(value):
        return value.astype(BF16)

    def join(value, more):
        return jnp.concatenate([value, more], 0)

    ma, mb, mc, md = steps
    part = half // 2

    def both(one, two):
        values = lax.optimization_barrier((one[0], two[0]))
        return lax.optimization_barrier((send(values[0], one[1]), send(values[1], two[1])))

    def around(value, left):
        for step in left:
            value = value + send(narrow(value), step)
        mine = narrow(value)
        mine = join(mine, send(mine, ma))
        return value, (mine, send(mine, core))

    def everywhere(value, sent):
        value = value + send(sent, core)
        value = value[:part] + send(narrow(value[part:]), ma)
        return around(value, (mb, mc, md))

    h = narrow(start_block[:HB, 1])
    more = send(h, md)
    l1, a, sent = first()
    h = join(h, more)
    more, got = both((h, mc), (sent, core))
    h, a = join(h, more), a + got
    more = send(h, mb)
    h = join(h, more)
    a = a[:part] + send(narrow(a[part:]), ma)
    h = join(h, send(h, ma))
    a, ta = around(a, (mb, mc, md))
    h = (h, send(h, core))
    base, l2, b, sent = middle(1, start_block, h, start_block, REL, OWN_REL, ABS, OWN_ABS, "second")
    b, tb = everywhere(b, sent)
    base, l3, c, sent = middle(2, l1, ta, base, ABS, OWN_ABS, ABS, OWN_ABS, "third")
    c, tc = everywhere(c, sent)
    base, l4, d, sent = middle(3, l2, tb, base, ABS, OWN_ABS, REL, OWN_REL, "fourth")
    d = d + send(sent, core)
    for step in steps:
        size = d.shape[0] // 2
        d = d[:size] + send(narrow(d[size:]), step)
    return last(l3, tc, base, l4, (a, b, c, d))


def solution(mesh):
    placed = (
        P("rows", None, None, None),
        P("rows", None),
        P("rows"),
        P("rows", None, None, None),
        P("dom"),
        P("dom"),
    )
    return jax.shard_map(
        body,
        mesh=mesh,
        in_specs=placed,
        out_specs=P(("dom", "rows"), None, None, None),
        check_vma=False,
    )
```
